128 devices in a mesh: seg: 64 (over y, z, x_hi, core), blk: 2 (over x_lo).
Axes of the slice: x: 4 (x_hi: 2, x_lo: 2; x = x_hi * 2 + x_lo), y: 4, z: 4, core: 2. Of those that a mesh axis runs over, the one named last changes fastest.
Arguments:
- state: bfloat16 [64, 4, 128, 2048], P('seg', 'blk'), may hold values from -6 to 6
- left_env: bfloat16 [64, 14, 4, 128, 128], P('seg', None, 'blk'), may hold values from -5 to 5
- right_env: bfloat16 [64, 14, 4, 128, 128], P('seg', None, 'blk'), may hold values from -3 to 3
- site_ops: bfloat16 [64, 14, 16, 16], P('seg'), may hold values from -4 to 4
- sector_map: int32 [64, 14, 4], P('seg'), may hold values from 0 to 3, as said below
- ranks: int32 [64, 4], P('seg', 'blk'), may hold values from 1 to 128
Outputs:
- new_state: bfloat16 [64, 4, 128, 2048], P('seg', 'blk')
- from_left: float32 [64, 14, 4, 128, 128], P('seg', None, 'blk')
- from_right: float32 [64, 14, 4, 128, 128], P('seg', None, 'blk')
The draws below stay inside these ranges and needn't reach their ends.
Inputs may be any that keep to these rules, and one draw needn't show every extreme that they name: `sector_map`: channel 0 carries every block into itself; the other channels' source blocks are arbitrary.
All inputs are finite; a program needn't handle non-finite values.
Results may differ from the reference program's by a relative error of at most 0.012.
Values may be sent and summed in bfloat16 or wider, within the bound.
A program may use at most 192 MiB of HBM per device.

```python
import math
import jax
import jax.numpy as jnp
from jax import lax

BLK = 128
PHYS2 = 16
CHAN = 14
NB = 4
SEGS = 64


def draw_left_env(key, part):
    key = jax.random.fold_in(key, 11)
    jitter_key, scale_key = jax.random.split(key)
    array_shape = (SEGS, CHAN, NB, BLK, BLK)
    jitter = jnp.clip(jax.random.normal(jitter_key, array_shape, jnp.float32), -4.0, 4.0)
    factor = jnp.exp(jax.random.uniform(scale_key, (SEGS, NB), jnp.float32, math.log(0.6), 0.0))
    jitter = jitter / math.sqrt(BLK)
    position = jnp.arange(NB, dtype=jnp.float32) / max(NB - 1, 1)
    gain_rows = jnp.exp(math.log(3.0) * position)[None, :] * factor
    identity = jnp.eye(BLK, dtype=jnp.float32)
    channel_zero = gain_rows[:, :, None, None] * (identity[None, None] + 0.5 * jitter[:, 0])
    return jnp.concatenate([channel_zero[:, None], jitter[:, 1:]], axis=1).astype(jnp.bfloat16)


def draw_right_env(key, part):
    key = jax.random.fold_in(key, 12)
    jitter_key, scale_key = jax.random.split(key)
    array_shape = (SEGS, CHAN, NB, BLK, BLK)
    jitter = jnp.clip(jax.random.normal(jitter_key, array_shape, jnp.float32), -4.0, 4.0)
    factor = jnp.exp(jax.random.uniform(scale_key, (SEGS, NB), jnp.float32, math.log(0.7), math.log(1.4)))
    jitter = jitter / math.sqrt(BLK)
    identity = jnp.eye(BLK, dtype=jnp.float32)
    channel_zero = factor[:, :, None, None] * (identity[None, None] + 0.5 * jitter[:, 0])
    return jnp.concatenate([channel_zero[:, None], jitter[:, 1:]], axis=1).astype(jnp.bfloat16)


def draw_site_ops(key, part):
    key = jax.random.fold_in(key, 13)
    jitter_key, level_key, spread_key = jax.random.split(key, 3)
    array_shape = (SEGS, CHAN, PHYS2, PHYS2)
    jitter = jnp.clip(jax.random.normal(jitter_key, array_shape, jnp.float32), -4.0, 4.0)
    jitter = jitter / math.sqrt(PHYS2)
    level = jax.random.uniform(level_key, (SEGS,), jnp.float32, 1.0, 2.0)
    spread = jax.random.uniform(spread_key, (SEGS, PHYS2), jnp.float32, 0.0, 1.0)
    identity = jnp.eye(PHYS2, dtype=jnp.float32)
    diagonal = (level[:, None] + spread)[:, :, None] * identity[None]
    channel_zero = diagonal + 0.5 * jitter[:, 0]
    return jnp.concatenate([channel_zero[:, None], jitter[:, 1:]], axis=1).astype(jnp.bfloat16)


def draw_sector_map(key, part):
    key = jax.random.fold_in(key, 14)
    sources = jax.random.randint(key, (SEGS, CHAN, NB), 0, NB, dtype=jnp.int32)
    own_blocks = jnp.broadcast_to(jnp.arange(NB, dtype=jnp.int32)[None, None, :], (SEGS, 1, NB))
    return jnp.concatenate([own_blocks, sources[:, 1:]], axis=1)


def place_ends(entries, key, least, top_value):
    spot = [jax.random.randint(jax.random.fold_in(key, axis), (), 0, length) for axis, length in enumerate(entries.shape)]
    widest = entries.shape.index(max(entries.shape))
    next_to = spot[:widest] + [(spot[widest] + 1) % entries.shape[widest]] + spot[widest + 1:]
    return entries.at[tuple(spot)].set(least).at[tuple(next_to)].set(top_value)


def level_of(key, extent, shards, low, high):
    def one(dim, parts):
        heights = jax.random.uniform(jax.random.fold_in(jax.random.fold_in(key, 6), dim), (parts,), jnp.float32, low / len(shards), high / len(shards))
        return jnp.repeat(jnp.exp(heights), extent[dim] // parts).reshape((-1,) + (1,) * (len(extent) - dim - 1))

    factor_of = one(*shards[0])
    for cut in shards[1:]:
        factor_of = factor_of * one(*cut)
    return factor_of


def noise(stream_key, shape, width, limit, cuts=(), kind=jnp.bfloat16):
    gain = level_of(stream_key, shape, cuts, -0.22, 0.18) if cuts else 1.0
    array = jax.random.normal(stream_key, shape, jnp.float32) * width * gain
    return jnp.minimum(jnp.maximum(array, -limit), limit).astype(kind)


def setup_inputs(seed: int = 0) -> dict:
    arg_keys = jax.random.split(jax.random.key(seed), 7)
    return {
        "state": noise(arg_keys[0], (SEGS, NB, BLK, PHYS2 * BLK), 1.0, 6.0, ((0, 64), (1, 2))),
        "left_env": draw_left_env(jax.random.fold_in(arg_keys[6], 71), 0),
        "right_env": draw_right_env(jax.random.fold_in(arg_keys[6], 71), 0),
        "site_ops": draw_site_ops(jax.random.fold_in(arg_keys[6], 71), 0),
        "sector_map": draw_sector_map(jax.random.fold_in(arg_keys[6], 71), 0),
        "ranks": place_ends(jax.random.randint(arg_keys[5], (SEGS, NB), 1, BLK + 1), jax.random.fold_in(arg_keys[5], 1), 1, BLK).astype(jnp.int32),
    }


STEP_SIZE = 0.25
EPSILON = 1e-06

def apply_hamiltonian(vector, left_env, right_env, site_ops, sector_map):
    blocks = vector.reshape(NB, BLK, PHYS2, BLK)
    sources = blocks[sector_map.astype(jnp.int32)]
    mixed_ops = jnp.einsum('kpq,kbaqc->kbapc', site_ops.astype(jnp.float32), sources.astype(jnp.float32)).astype(jnp.bfloat16)
    left_part = jnp.einsum('kbxa,kbapc->kbxpc', left_env.astype(jnp.float32), mixed_ops.astype(jnp.float32)).astype(jnp.bfloat16)
    result = jnp.einsum('kbcd,kbapd->bapc', right_env.astype(jnp.float32), left_part.astype(jnp.float32))
    return result.reshape(NB, BLK, PHYS2 * BLK)

def segment_update(packed):
    state, left_env, right_env, site_ops, sector_map, ranks = packed
    image_rows = apply_hamiltonian(state, left_env, right_env, site_ops, sector_map)
    state_float = state.astype(jnp.float32)
    energy_one = jnp.sum(state_float * image_rows) / jnp.sum(state_float * state_float)
    first_step = (state_float - STEP_SIZE * (image_rows - energy_one * state_float)).astype(jnp.bfloat16)
    image_next = apply_hamiltonian(first_step, left_env, right_env, site_ops, sector_map)
    first_float = first_step.astype(jnp.float32)
    energy_two = jnp.sum(first_float * image_next) / jnp.sum(first_float * first_float)
    keep_mask = (jnp.arange(BLK, dtype=jnp.int32)[None, :] < ranks.astype(jnp.int32)[:, None]).astype(jnp.float32)[:, :, None]
    kept_part = keep_mask * (first_float - STEP_SIZE * (image_next - energy_two * first_float))
    norm_square = jnp.sum(kept_part * kept_part)
    total_cells = jnp.float32(NB * BLK * PHYS2 * BLK)
    new_state = (kept_part * jnp.sqrt(total_cells / (norm_square + EPSILON))).astype(jnp.bfloat16)
    state_four = new_state.reshape(NB, BLK, PHYS2, BLK).astype(jnp.float32)
    env_scale = 1.0 / math.sqrt(PHYS2 * BLK)
    left_mixed = jnp.einsum('kbxa,bapc->kbxpc', left_env.astype(jnp.float32), state_four).astype(jnp.bfloat16)
    left_new = jnp.einsum('bxpc,kbxpd->kbcd', state_four, left_mixed.astype(jnp.float32)) * env_scale
    right_mixed = jnp.einsum('kbcd,bapd->kbapc', right_env.astype(jnp.float32), state_four).astype(jnp.bfloat16)
    right_new = jnp.einsum('bapc,kbxpc->kbax', state_four, right_mixed.astype(jnp.float32)) * env_scale
    return (new_state, left_new, right_new)

def reference(state, left_env, right_env, site_ops, sector_map, ranks):
    new_state, left_new, right_new = lax.map(segment_update, (state, left_env, right_env, site_ops, sector_map, ranks))
    from_left = jnp.concatenate([jnp.zeros_like(left_new[:1]), left_new[:-1]], axis=0)
    from_right = jnp.concatenate([right_new[1:], jnp.zeros_like(right_new[:1])], axis=0)
    return (new_state, from_left, from_right)
```

```python
import functools
import math

import jax
import jax.numpy as jnp
from jax import lax
from jax.experimental import pallas as pl
from jax.experimental.pallas import tpu as pltpu
from jax.sharding import PartitionSpec as P

STEP_SIZE = 0.25
EPSILON = 1e-06
MESH = pl.DeviceIdType.MESH
BF16 = jnp.bfloat16
F32 = jnp.float32


def dot(a, b):
    return jnp.dot(a, b, preferred_element_type=F32)


def kernel(dims, *refs):
    segs, chan, phys, blk, rows, chunks = dims
    wide = phys * blk
    tall = phys * rows
    pairs = chan // 2
    (state_ref, left_ref, right_ref, ops_ref, map_ref, ranks_ref, new_ref, recv_ref) = refs[:8]
    x = refs[8 : 8 + chunks]
    (env, lcat, kron, rdiag, z, img, wave, mixbuf, outbuf, sums, got) = refs[8 + chunks : 19 + chunks]
    (in_sem, own_sem, xs_sem, xr_sem, es_sem, er_sem, ss_sem, sr_sem) = refs[19 + chunks :]

    seg = lax.axis_index("seg")
    group = lax.axis_index("blk")
    other = 1 - group
    following = lax.rem(seg + 1, segs)
    previous = lax.rem(seg + segs - 1, segs)
    partner = (seg, other)

    own_copies = [
        pltpu.make_async_copy(
            state_ref.at[0, :, pl.ds(g * rows, rows), :], x[g].at[pl.ds(0, 2)], own_sem.at[g]
        )
        for g in range(chunks)
    ]
    left_copy = pltpu.make_async_copy(left_ref.at[0], env.at[0], in_sem.at[0])
    right_copy = pltpu.make_async_copy(right_ref.at[0], env.at[1], in_sem.at[1])
    barrier = pltpu.get_barrier_semaphore()
    for where in ((seg, other), (following, group), (previous, group)):
        pl.semaphore_signal(barrier, inc=1, device_id=where, device_id_type=MESH)
    right_copy.start()
    left_copy.start()
    for copy in own_copies:
        copy.start()
    pl.semaphore_wait(barrier, 3)

    def exchange(g, source):
        return pltpu.make_async_remote_copy(
            src_ref=source,
            dst_ref=x[g].at[pl.ds(2, 2)],
            send_sem=xs_sem.at[g],
            recv_sem=xr_sem.at[g],
            device_id=partner,
            device_id_type=MESH,
        )

    sends = [exchange(g, state_ref.at[0, :, pl.ds(g * rows, rows), :]) for g in range(chunks)]
    for copy in sends:
        copy.start()

    line = lax.broadcasted_iota(jnp.int32, (tall, phys), 0)
    pick = lax.broadcasted_iota(jnp.int32, (tall, phys), 1)
    spread_rows = (line // rows == pick).astype(BF16)
    line = lax.broadcasted_iota(jnp.int32, (phys, tall), 1)
    pick = lax.broadcasted_iota(jnp.int32, (phys, tall), 0)
    spread_cols = (line // rows == pick).astype(BF16)
    same = lax.broadcasted_iota(jnp.int32, (tall, tall), 0) % rows == (
        lax.broadcasted_iota(jnp.int32, (tall, tall), 1) % rows
    )

    def build_kron(k, carry):
        tall_op = dot(spread_rows, ops_ref[0, k]).astype(BF16)
        full = dot(tall_op, spread_cols)
        kron[k] = jnp.where(same, full, 0.0).astype(BF16)
        return carry

    lax.fori_loop(0, chan, build_kron, 0)

    right_copy.wait()

    def build_rdiag(k, carry):
        zeros = jnp.zeros((blk, blk), BF16)
        for b in range(2):
            turned = env[1, k, b].astype(F32).T.astype(BF16)
            rdiag[k, b * blk : (b + 1) * blk, b * blk : (b + 1) * blk] = turned
            rdiag[k, b * blk : (b + 1) * blk, (1 - b) * blk : (2 - b) * blk] = zeros
        return carry

    lax.fori_loop(0, chan, build_rdiag, 0)

    left_copy.wait()
    for k in range(chan):
        for b in range(2):
            lcat[b, :, k * blk : (k + 1) * blk] = env[0, k, b]

    def tiles(slab):
        return [slab[:, p * blk : (p + 1) * blk] for p in range(phys)]

    def contract(g):
        def one(k, carry):
            spots = [
                lax.rem(map_ref[0, k, 2 * group + b] + 4 - 2 * group, 4) for b in range(2)
            ]
            source = jnp.concatenate(
                [jnp.concatenate(tiles(x[g][spot]), axis=0) for spot in spots], axis=1
            )
            mixed = dot(kron[k], source).astype(BF16)
            part = dot(mixed, rdiag[k]).astype(BF16)
            row = pl.multiple_of(k * blk + g * rows, rows)
            for b in range(2):
                for p in range(phys):
                    z[b, pl.ds(row, rows), p * blk : (p + 1) * blk] = part[
                        p * rows : (p + 1) * rows, b * blk : (b + 1) * blk
                    ]
            return carry

        lax.fori_loop(0, chan, one, 0, unroll=2)

    def finish_image():
        for b in range(2):

            def one(n, carry):
                cols = pl.ds(pl.multiple_of(n * 256, 256), 256)
                img[b, :, cols] = dot(lcat[b], z[b, :, cols])
                return carry

            lax.fori_loop(0, wide // 256, one, 0)

    def fold(product):
        both = product[0] + product[1]
        total = both[:, :blk]
        for p in range(1, phys):
            total = total + both[:, p * blk : (p + 1) * blk]
        return total

    def rows_of(g):
        return slice(g * rows, (g + 1) * rows)

    def pair_total(slot, parts):
        for i, part in enumerate(parts):
            sums[slot, i] = part
        count = len(parts)
        copy = pltpu.make_async_remote_copy(
            src_ref=sums.at[slot, pl.ds(0, count)],
            dst_ref=got.at[slot, pl.ds(0, count)],
            send_sem=ss_sem.at[slot],
            recv_sem=sr_sem.at[slot],
            device_id=partner,
            device_id_type=MESH,
        )
        copy.start()
        copy.wait()
        return [
            jnp.sum(parts[i] + got[slot, i], axis=(0, 1), keepdims=True) for i in range(count)
        ]

    for g in range(chunks):
        own_copies[g].wait()
        sends[g].wait_recv()
        contract(g)
    finish_image()
    num = jnp.zeros((rows, blk), F32)
    den = jnp.zeros((rows, blk), F32)
    for g in range(chunks):
        own = x[g][0:2].astype(F32)
        num = num + fold(own * img[:, rows_of(g), :])
        den = den + fold(own * own)
    num, den = pair_total(0, [num, den])
    energy_one = num / den

    for copy in sends:
        copy.wait_send()
    den = jnp.zeros((rows, blk), F32)
    sends = [exchange(g, x[g].at[pl.ds(0, 2)]) for g in range(chunks)]
    for g in range(chunks):
        own = x[g][0:2].astype(F32)
        first = (own - STEP_SIZE * (img[:, rows_of(g), :] - energy_one * own)).astype(BF16)
        x[g][0:2] = first
        sends[g].start()
        first = first.astype(F32)
        den = den + fold(first * first)

    for g in range(chunks):
        sends[g].wait_recv()
        contract(g)
    finish_image()
    num = jnp.zeros((rows, blk), F32)
    for g in range(chunks):
        num = num + fold(x[g][0:2].astype(F32) * img[:, rows_of(g), :])
    num, den = pair_total(1, [num, den])
    energy_two = num / den

    norm = jnp.zeros((rows, blk), F32)
    for g in range(chunks):
        line = g * rows + lax.broadcasted_iota(jnp.int32, (rows, wide), 0)
        first = x[g][0:2].astype(F32)
        kept = first - STEP_SIZE * (img[:, rows_of(g), :] - energy_two * first)
        kept = jnp.stack(
            [jnp.where(line < ranks_ref[0, b], kept[b], 0.0) for b in range(2)], axis=0
        )
        img[:, rows_of(g), :] = kept
        norm = norm + fold(kept * kept)
    (norm,) = pair_total(2, [norm])
    cells = float(4 * blk * wide)
    scale = jnp.sqrt(cells / (norm + EPSILON))
    for b in range(2):

        def turn(p, carry):
            cols = pl.ds(pl.multiple_of(p * blk, blk), blk)
            tile = img[b, :, cols] * scale
            rounded = tile.astype(BF16)
            wave[0, b, :, cols] = rounded
            wave[1, b, :, cols] = tile.T.astype(BF16)
            return carry

        lax.fori_loop(0, phys, turn, 0, unroll=2)
    new_copy = pltpu.make_async_copy(wave.at[0], new_ref.at[0], in_sem.at[2])
    new_copy.start()

    env_scale = 1.0 / math.sqrt(wide)
    first_side = 1 - lax.rem(seg, 2)

    def boundary(side, pair):
        channels = pl.ds(2 * pair, 2)
        target = lax.rem(seg + 1 - 2 * side + segs, segs)
        return pltpu.make_async_remote_copy(
            src_ref=outbuf.at[side, channels],
            dst_ref=recv_ref.at[side, channels],
            send_sem=es_sem.at[side, pair],
            recv_sem=er_sem.at[side, pair],
            device_id=(target, group),
            device_id_type=MESH,
        )

    for turn_index in range(2):
        side = first_side if turn_index == 0 else 1 - first_side

        def one_pair(pair, carry):
            for b in range(2):
                ends = jnp.concatenate([env[side, 2 * pair, b], env[side, 2 * pair + 1, b]], axis=0)
                for n in range(phys // 2):
                    part = dot(ends, wave[side, b, :, 2 * n * blk : (2 * n + 2) * blk]).astype(BF16)
                    for i in range(2):
                        for j in range(2):
                            mixbuf[
                                b,
                                (2 * n + j) * blk : (2 * n + j + 1) * blk,
                                i * blk : (i + 1) * blk,
                            ] = part[i * blk : (i + 1) * blk, j * blk : (j + 1) * blk]
            for b in range(2):
                result = (dot(wave[1 - side, b], mixbuf[b]) * env_scale).astype(BF16)
                for i in range(2):
                    outbuf[side, 2 * pair + i, b] = result[:, i * blk : (i + 1) * blk]
            boundary(side, pair).start()
            return carry

        lax.fori_loop(0, pairs, one_pair, 0)

    for copy in sends:
        copy.wait_send()
    new_copy.wait()

    def settle(pair, carry):
        for side in range(2):
            boundary(side, pair).wait()
        return carry

    lax.fori_loop(0, pairs, settle, 0)


def solution(mesh):
    segs = mesh.shape["seg"]

    def shards(state, left_env, right_env, site_ops, sector_map, ranks):
        chan, _, blk, _ = left_env.shape[1:]
        phys = site_ops.shape[2]
        rows = 16
        chunks = blk // rows
        wide = phys * blk
        dims = (segs, chan, phys, blk, rows, chunks)
        anywhere = pl.BlockSpec(memory_space=pl.ANY)
        in_vmem = pl.BlockSpec(memory_space=pltpu.VMEM)
        in_smem = pl.BlockSpec(memory_space=pltpu.SMEM)
        dma = pltpu.SemaphoreType.DMA
        new_state, received = pl.pallas_call(
            functools.partial(kernel, dims),
            out_shape=(
                jax.ShapeDtypeStruct(state.shape, BF16),
                jax.ShapeDtypeStruct((2, chan, 2, blk, blk), BF16),
            ),
            in_specs=[anywhere, anywhere, anywhere, in_vmem, in_smem, in_smem],
            out_specs=(anywhere, anywhere),
            scratch_shapes=[pltpu.VMEM((4, rows, wide), BF16) for _ in range(chunks)]
            + [
                pltpu.VMEM((2, chan, 2, blk, blk), BF16),
                pltpu.VMEM((2, blk, chan * blk), BF16),
                pltpu.VMEM((chan, phys * rows, phys * rows), BF16),
                pltpu.VMEM((chan, 2 * blk, 2 * blk), BF16),
                pltpu.VMEM((2, chan * blk, wide), BF16),
                pltpu.VMEM((2, blk, wide), F32),
                pltpu.VMEM((2, 2, blk, wide), BF16),
                pltpu.VMEM((2, wide, 2 * blk), BF16),
                pltpu.VMEM((2, chan, 2, blk, blk), BF16),
                pltpu.VMEM((3, 2, rows, blk), F32),
                pltpu.VMEM((3, 2, rows, blk), F32),
                dma((3,)),
                dma((chunks,)),
                dma((chunks,)),
                dma((chunks,)),
                dma((2, chan // 2)),
                dma((2, chan // 2)),
                dma((3,)),
                dma((3,)),
            ],
            compiler_params=pltpu.CompilerParams(
                collective_id=0, has_side_effects=True, vmem_limit_bytes=60 * 1024 * 1024
            ),
        )(state, left_env, right_env, site_ops, sector_map, ranks)
        seg = lax.axis_index("seg")
        from_left = jnp.where(seg == 0, 0.0, received[0].astype(F32))
        from_right = jnp.where(seg == segs - 1, 0.0, received[1].astype(F32))
        return (new_state, from_left[None], from_right[None])

    placed = (
        P("seg", "blk", None, None),
        P("seg", None, "blk", None, None),
        P("seg", None, "blk", None, None),
        P("seg", None, None, None),
        P("seg", None, None),
        P("seg", "blk"),
    )
    return jax.shard_map(
        shards,
        mesh=mesh,
        in_specs=placed,
        out_specs=(
            P("seg", "blk", None, None),
            P("seg", None, "blk", None, None),
            P("seg", None, "blk", None, None),
        ),
        check_vma=False,
    )
```

```python
import functools
import math

import jax
import jax.numpy as jnp
from jax import lax
from jax.experimental import pallas as pl
from jax.experimental.pallas import tpu as pltpu
from jax.sharding import PartitionSpec as P

STEP_SIZE = 0.25
EPSILON = 1e-06
MESH = pl.DeviceIdType.MESH
BF16 = jnp.bfloat16
F32 = jnp.float32


def dot(a, b):
    return jnp.dot(a, b, preferred_element_type=F32)


def kernel(dims, *refs):
    segs, chan, phys, blk, rows, chunks = dims
    wide = phys * blk
    tall = phys * rows
    pairs = chan // 2
    (state_ref, left_ref, right_ref, ops_in, map_in, ranks_in, new_ref, recv_ref) = refs[:8]
    x = refs[8 : 8 + chunks]
    y = refs[8 + chunks : 8 + 2 * chunks]
    rest = refs[8 + 2 * chunks :]
    (env, lcat, kron, rdiag, z, img, imgb, wave, mixbuf, outbuf, sums, got) = rest[:12]
    (ops_ref, map_ref, ranks_ref) = rest[12:15]
    (in_sem, own_sem, xs_sem, xr_sem, ys_sem, yr_sem, es_sem, er_sem, ss_sem, sr_sem) = rest[15:]

    seg = lax.axis_index("seg")
    group = lax.axis_index("blk")
    other = 1 - group
    following = lax.rem(seg + 1, segs)
    previous = lax.rem(seg + segs - 1, segs)
    partner = (seg, other)

    own_copies = [
        pltpu.make_async_copy(
            state_ref.at[0, :, pl.ds(g * rows, rows), :], x[g].at[pl.ds(0, 2)], own_sem.at[g]
        )
        for g in range(chunks)
    ]
    left_copy = pltpu.make_async_copy(left_ref.at[0], env.at[0], in_sem.at[0])
    right_copy = pltpu.make_async_copy(right_ref.at[0], env.at[1], in_sem.at[1])
    barrier = pltpu.get_barrier_semaphore()
    for where in ((seg, other), (following, group), (previous, group)):
        pl.semaphore_signal(barrier, inc=1, device_id=where, device_id_type=MESH)
    ops_copy = pltpu.make_async_copy(ops_in.at[0], ops_ref, in_sem.at[3])
    map_copy = pltpu.make_async_copy(map_in, map_ref, in_sem.at[4])
    ranks_copy = pltpu.make_async_copy(ranks_in, ranks_ref, in_sem.at[5])
    for copy in [ops_copy, right_copy, left_copy, map_copy, ranks_copy] + own_copies:
        copy.start()
    pl.semaphore_wait(barrier, 3)

    def exchange(g):
        return pltpu.make_async_remote_copy(
            src_ref=state_ref.at[0, :, pl.ds(g * rows, rows), :],
            dst_ref=x[g].at[pl.ds(2, 2)],
            send_sem=xs_sem.at[g],
            recv_sem=xr_sem.at[g],
            device_id=partner,
            device_id_type=MESH,
        )

    def exchange_image(b, g):
        return pltpu.make_async_remote_copy(
            src_ref=imgb.at[b, pl.ds(g * rows, rows), :],
            dst_ref=y[g].at[b],
            send_sem=ys_sem.at[b, g],
            recv_sem=yr_sem.at[b, g],
            device_id=partner,
            device_id_type=MESH,
        )

    sends = [exchange(g) for g in range(chunks)]
    for copy in sends:
        copy.start()

    line = lax.broadcasted_iota(jnp.int32, (tall, phys), 0)
    pick = lax.broadcasted_iota(jnp.int32, (tall, phys), 1)
    spread_rows = (line // rows == pick).astype(BF16)
    line = lax.broadcasted_iota(jnp.int32, (phys, tall), 1)
    pick = lax.broadcasted_iota(jnp.int32, (phys, tall), 0)
    spread_cols = (line // rows == pick).astype(BF16)
    same = lax.broadcasted_iota(jnp.int32, (tall, tall), 0) % rows == (
        lax.broadcasted_iota(jnp.int32, (tall, tall), 1) % rows
    )

    ops_copy.wait()

    def build_kron(k, carry):
        tall_op = dot(spread_rows, ops_ref[k]).astype(BF16)
        full = dot(tall_op, spread_cols)
        kron[k] = jnp.where(same, full, 0.0).astype(BF16)
        return carry

    lax.fori_loop(0, chan, build_kron, 0)

    right_copy.wait()

    def build_rdiag(k, carry):
        zeros = jnp.zeros((blk, blk), BF16)
        for b in range(2):
            turned = env[1, k, b].astype(F32).T.astype(BF16)
            rdiag[k, b * blk : (b + 1) * blk, b * blk : (b + 1) * blk] = turned
            rdiag[k, b * blk : (b + 1) * blk, (1 - b) * blk : (2 - b) * blk] = zeros
        return carry

    lax.fori_loop(0, chan, build_rdiag, 0)

    map_copy.wait()
    ranks_copy.wait()
    left_copy.wait()
    for k in range(chan):
        for b in range(2):
            lcat[b, :, k * blk : (k + 1) * blk] = env[0, k, b]

    def tiles(slab):
        return [slab[:, p * blk : (p + 1) * blk] for p in range(phys)]

    def contract(g):
        def one(k, carry):
            spots = [
                lax.rem(map_ref[0, 2 * group + b, k] + 4 - 2 * group, 4) for b in range(2)
            ]
            source = jnp.concatenate(
                [jnp.concatenate(tiles(x[g][spot]), axis=0) for spot in spots], axis=1
            )
            mixed = dot(kron[k], source).astype(BF16)
            part = dot(mixed, rdiag[k]).astype(BF16)
            row = pl.multiple_of(k * blk + g * rows, rows)
            for b in range(2):
                for p in range(phys):
                    z[b, pl.ds(row, rows), p * blk : (p + 1) * blk] = part[
                        p * rows : (p + 1) * rows, b * blk : (b + 1) * blk
                    ]
            return carry

        lax.fori_loop(0, chan, one, 0, unroll=2)

    def finish_image(b, num, keep_rounded):
        def one(n, carry):
            start = pl.multiple_of(n * 256, 256)
            cols = pl.ds(start, 256)
            tile = dot(lcat[b], z[b, :, cols])
            img[b, :, cols] = tile
            if keep_rounded:
                imgb[b, :, cols] = tile.astype(BF16)
            for g in range(chunks):
                part = x[g][b, :, cols].astype(F32) * tile[g * rows : (g + 1) * rows, :]
                carry = carry + part[:, :blk] + part[:, blk:]
            return carry

        return lax.fori_loop(0, wide // 256, one, num)

    def fold(product):
        both = product[0] + product[1]
        total = both[:, :blk]
        for p in range(1, phys):
            total = total + both[:, p * blk : (p + 1) * blk]
        return total

    def rows_of(g):
        return slice(g * rows, (g + 1) * rows)

    def send_sums(slot, parts):
        for i, part in enumerate(parts):
            sums[slot, i] = part
        copy = pltpu.make_async_remote_copy(
            src_ref=sums.at[slot, pl.ds(0, len(parts))],
            dst_ref=got.at[slot, pl.ds(0, len(parts))],
            send_sem=ss_sem.at[slot],
            recv_sem=sr_sem.at[slot],
            device_id=partner,
            device_id_type=MESH,
        )
        copy.start()
        return copy

    def total_of(part):
        return jnp.sum(part, axis=(0, 1), keepdims=True)

    den = jnp.zeros((rows, blk), F32)
    for g in range(chunks):
        own_copies[g].wait()
        own = x[g][0:2].astype(F32)
        den = den + fold(own * own)
        sends[g].wait_recv()
        contract(g)
    num = finish_image(0, jnp.zeros((rows, blk), F32), True)
    images = [[exchange_image(b, g) for g in range(chunks)] for b in range(2)]
    for g in range(2):
        images[0][g].start()
    num = finish_image(1, num, True)
    message = send_sums(0, [num, den])
    for g in range(2):
        images[1][g].start()
    for g in range(2, chunks):
        for b in range(2):
            images[b][g].start()
    message.wait()
    energy_one = total_of(num + got[0, 0]) / total_of(den + got[0, 1])

    den = jnp.zeros((rows, blk), F32)
    for g in range(chunks):
        own = x[g][0:2].astype(F32)
        first = (own - STEP_SIZE * (img[:, rows_of(g), :] - energy_one * own)).astype(BF16)
        x[g][0:2] = first
        first = first.astype(F32)
        den = den + fold(first * first)

    for g in range(chunks):
        for b in range(2):
            images[b][g].wait_recv()
        theirs = x[g][2:4].astype(F32)
        x[g][2:4] = (theirs - STEP_SIZE * (y[g][...].astype(F32) - energy_one * theirs)).astype(BF16)
        contract(g)
    num = jnp.zeros((rows, blk), F32)
    for b in range(2):
        num = finish_image(b, num, False)

    def quotient(top, bottom):
        top, bottom = total_of(top), total_of(bottom)
        return jnp.where(bottom > 0.0, top / bottom, 0.0)

    near = quotient(num, den)
    square = jnp.zeros((rows, blk), F32)
    cross = jnp.zeros((rows, blk), F32)
    start = jnp.zeros((rows, blk), F32)
    for g in range(chunks):
        line = g * rows + lax.broadcasted_iota(jnp.int32, (rows, wide), 0)
        first = x[g][0:2].astype(F32)
        first = jnp.stack(
            [jnp.where(line < ranks_ref[0, b], first[b], 0.0) for b in range(2)], axis=0
        )
        image = jnp.stack(
            [jnp.where(line < ranks_ref[0, b], img[b, rows_of(g), :], 0.0) for b in range(2)], axis=0
        )
        kept = first - STEP_SIZE * (image - near * first)
        img[:, rows_of(g), :] = kept
        square = square + fold(kept * kept)
        cross = cross + fold(kept * first)
        start = start + fold(first * first)
    send_sums(1, [num, den, square, cross, start]).wait()
    energy_two = total_of(num + got[1, 0]) / total_of(den + got[1, 1])

    def square_at(step, a, b, c):
        return total_of(a) + step * (0.5 * total_of(b) + 0.0625 * (step * total_of(c)))

    shift = energy_two - near
    far = energy_two - quotient(got[1, 0], got[1, 1])
    norm = square_at(shift, square, cross, start) + square_at(far, got[1, 2], got[1, 3], got[1, 4])
    norm = jnp.maximum(norm, 0.0)
    cells = float(4 * blk * wide)
    scale = jnp.sqrt(cells / (norm + EPSILON))
    for b in range(2):
        inside = lax.broadcasted_iota(jnp.int32, (blk, blk), 0) < ranks_ref[0, b]

        def turn(p, carry):
            cols = pl.ds(pl.multiple_of(p * blk, blk), blk)
            first = jnp.concatenate([x[g][b, :, cols] for g in range(chunks)], axis=0)
            first = jnp.where(inside, first.astype(F32), 0.0)
            tile = (img[b, :, cols] + (STEP_SIZE * shift) * first) * scale
            wave[0, b, :, cols] = tile.astype(BF16)
            wave[1, b, :, cols] = tile.T.astype(BF16)
            return carry

        lax.fori_loop(0, phys, turn, 0, unroll=2)
    new_copy = pltpu.make_async_copy(wave.at[0], new_ref.at[0], in_sem.at[2])
    new_copy.start()

    env_scale = 1.0 / math.sqrt(wide)
    first_side = 1 - lax.rem(seg, 2)

    def boundary(side, pair):
        channels = pl.ds(2 * pair, 2)
        target = lax.rem(seg + 1 - 2 * side + segs, segs)
        return pltpu.make_async_remote_copy(
            src_ref=outbuf.at[side, channels],
            dst_ref=recv_ref.at[side, channels],
            send_sem=es_sem.at[side, pair],
            recv_sem=er_sem.at[side, pair],
            device_id=(target, group),
            device_id_type=MESH,
        )

    for turn_index in range(2):
        side = first_side if turn_index == 0 else 1 - first_side

        def one_pair(pair, carry):
            for b in range(2):
                ends = jnp.concatenate([env[side, 2 * pair, b], env[side, 2 * pair + 1, b]], axis=0)
                for n in range(phys // 2):
                    part = dot(ends, wave[side, b, :, 2 * n * blk : (2 * n + 2) * blk]).astype(BF16)
                    for i in range(2):
                        for j in range(2):
                            mixbuf[
                                b,
                                (2 * n + j) * blk : (2 * n + j + 1) * blk,
                                i * blk : (i + 1) * blk,
                            ] = part[i * blk : (i + 1) * blk, j * blk : (j + 1) * blk]
            for b in range(2):
                result = (dot(wave[1 - side, b], mixbuf[b]) * env_scale).astype(BF16)
                for i in range(2):
                    outbuf[side, 2 * pair + i, b] = result[:, i * blk : (i + 1) * blk]
            boundary(side, pair).start()
            return carry

        lax.fori_loop(0, pairs, one_pair, 0)

    for copy in sends + images[0] + images[1]:
        copy.wait_send()
    new_copy.wait()

    def settle(pair, carry):
        for side in range(2):
            boundary(side, pair).wait()
        return carry

    lax.fori_loop(0, pairs, settle, 0)


def solution(mesh):
    segs = mesh.shape["seg"]

    def shards(state, left_env, right_env, site_ops, sector_map, ranks):
        chan, _, blk, _ = left_env.shape[1:]
        phys = site_ops.shape[2]
        rows = 16
        chunks = blk // rows
        wide = phys * blk
        dims = (segs, chan, phys, blk, rows, chunks)
        anywhere = pl.BlockSpec(memory_space=pl.ANY)
        dma = pltpu.SemaphoreType.DMA
        new_state, received = pl.pallas_call(
            functools.partial(kernel, dims),
            out_shape=(
                jax.ShapeDtypeStruct(state.shape, BF16),
                jax.ShapeDtypeStruct((2, chan, 2, blk, blk), BF16),
            ),
            in_specs=[anywhere] * 6,
            out_specs=(anywhere, anywhere),
            scratch_shapes=[pltpu.VMEM((4, rows, wide), BF16) for _ in range(chunks)]
            + [pltpu.VMEM((2, rows, wide), BF16) for _ in range(chunks)]
            + [
                pltpu.VMEM((2, chan, 2, blk, blk), BF16),
                pltpu.VMEM((2, blk, chan * blk), BF16),
                pltpu.VMEM((chan, phys * rows, phys * rows), BF16),
                pltpu.VMEM((chan, 2 * blk, 2 * blk), BF16),
                pltpu.VMEM((2, chan * blk, wide), BF16),
                pltpu.VMEM((2, blk, wide), F32),
                pltpu.VMEM((2, blk, wide), BF16),
                pltpu.VMEM((2, 2, blk, wide), BF16),
                pltpu.VMEM((2, wide, 2 * blk), BF16),
                pltpu.VMEM((2, chan, 2, blk, blk), BF16),
                pltpu.VMEM((2, 5, rows, blk), F32),
                pltpu.VMEM((2, 5, rows, blk), F32),
                pltpu.VMEM((chan, phys, phys), BF16),
                pltpu.SMEM((1, 4, chan), jnp.int32),
                pltpu.SMEM((1, 2), jnp.int32),
                dma((6,)),
                dma((chunks,)),
                dma((chunks,)),
                dma((chunks,)),
                dma((2, chunks)),
                dma((2, chunks)),
                dma((2, chan // 2)),
                dma((2, chan // 2)),
                dma((2,)),
                dma((2,)),
            ],
            compiler_params=pltpu.CompilerParams(
                collective_id=0, has_side_effects=True, vmem_limit_bytes=60 * 1024 * 1024
            ),
        )(state, left_env, right_env, site_ops, jnp.swapaxes(sector_map, 1, 2), ranks)
        seg = lax.axis_index("seg")
        from_left = jnp.where(seg == 0, 0.0, received[0].astype(F32))
        from_right = jnp.where(seg == segs - 1, 0.0, received[1].astype(F32))
        return (new_state, from_left[None], from_right[None])

    placed = (
        P("seg", "blk", None, None),
        P("seg", None, "blk", None, None),
        P("seg", None, "blk", None, None),
        P("seg", None, None, None),
        P("seg", None, None),
        P("seg", "blk"),
    )
    return jax.shard_map(
        shards,
        mesh=mesh,
        in_specs=placed,
        out_specs=(
            P("seg", "blk", None, None),
            P("seg", None, "blk", None, None),
            P("seg", None, "blk", None, None),
        ),
        check_vma=False,
    )
```

```python
import functools
import math

import jax
import jax.numpy as jnp
from jax import lax
from jax.experimental import pallas as pl
from jax.experimental.pallas import tpu as pltpu
from jax.sharding import PartitionSpec as P

STEP_SIZE = 0.25
EPSILON = 1e-06
MESH = pl.DeviceIdType.MESH
BF16 = jnp.bfloat16
F32 = jnp.float32


def dot(a, b):
    return jnp.dot(a, b, preferred_element_type=F32)


def kernel(dims, *refs):
    segs, chan, phys, blk, rows, chunks = dims
    wide = phys * blk
    tall = phys * rows
    pairs = chan // 2
    (state_ref, left_ref, right_ref, ops_in, map_in, ranks_in, new_ref, recv_ref) = refs[:8]
    x = refs[8 : 8 + chunks]
    y = refs[8 + chunks : 8 + 2 * chunks]
    rest = refs[8 + 2 * chunks :]
    (env, lcat, kron, rdiag, z, img, imgb, wave, mixbuf, outbuf, sums, got) = rest[:12]
    (ops_ref, map_ref, ranks_ref) = rest[12:15]
    (in_sem, own_sem, xs_sem, xr_sem, ys_sem, yr_sem, es_sem, er_sem, ss_sem, sr_sem) = rest[15:]

    seg = lax.axis_index("seg")
    group = lax.axis_index("blk")
    other = 1 - group
    following = lax.rem(seg + 1, segs)
    previous = lax.rem(seg + segs - 1, segs)
    partner = (seg, other)

    own_copies = [
        pltpu.make_async_copy(
            state_ref.at[0, :, pl.ds(g * rows, rows), :], x[g].at[pl.ds(0, 2)], own_sem.at[g]
        )
        for g in range(chunks)
    ]
    left_copy = pltpu.make_async_copy(left_ref.at[0], env.at[0], in_sem.at[0])
    right_copy = pltpu.make_async_copy(right_ref.at[0], env.at[1], in_sem.at[1])
    barrier = pltpu.get_barrier_semaphore()
    for where in ((seg, other), (following, group), (previous, group)):
        pl.semaphore_signal(barrier, inc=1, device_id=where, device_id_type=MESH)
    ops_copy = pltpu.make_async_copy(ops_in.at[0], ops_ref, in_sem.at[3])
    map_copy = pltpu.make_async_copy(map_in, map_ref, in_sem.at[4])
    ranks_copy = pltpu.make_async_copy(ranks_in, ranks_ref, in_sem.at[5])
    for copy in [ops_copy, right_copy, left_copy, map_copy, ranks_copy] + own_copies:
        copy.start()
    pl.semaphore_wait(barrier, 3)

    def exchange(g):
        return pltpu.make_async_remote_copy(
            src_ref=state_ref.at[0, :, pl.ds(g * rows, rows), :],
            dst_ref=x[g].at[pl.ds(2, 2)],
            send_sem=xs_sem.at[g],
            recv_sem=xr_sem.at[g],
            device_id=partner,
            device_id_type=MESH,
        )

    def exchange_image(b, g):
        return pltpu.make_async_remote_copy(
            src_ref=imgb.at[b, pl.ds(g * rows, rows), :],
            dst_ref=y[g].at[b],
            send_sem=ys_sem.at[b, g],
            recv_sem=yr_sem.at[b, g],
            device_id=partner,
            device_id_type=MESH,
        )

    sends = [exchange(g) for g in range(chunks)]
    for copy in sends:
        copy.start()

    line = lax.broadcasted_iota(jnp.int32, (tall, phys), 0)
    pick = lax.broadcasted_iota(jnp.int32, (tall, phys), 1)
    spread_rows = (line // rows == pick).astype(BF16)
    line = lax.broadcasted_iota(jnp.int32, (phys, tall), 1)
    pick = lax.broadcasted_iota(jnp.int32, (phys, tall), 0)
    spread_cols = (line // rows == pick).astype(BF16)
    same = lax.broadcasted_iota(jnp.int32, (tall, tall), 0) % rows == (
        lax.broadcasted_iota(jnp.int32, (tall, tall), 1) % rows
    )

    ops_copy.wait()

    def build_kron(k, carry):
        tall_op = dot(spread_rows, ops_ref[k]).astype(BF16)
        full = dot(tall_op, spread_cols)
        kron[k] = jnp.where(same, full, 0.0).astype(BF16)
        return carry

    lax.fori_loop(0, chan, build_kron, 0)

    right_copy.wait()

    def build_rdiag(k, carry):
        zeros = jnp.zeros((blk, blk), BF16)
        for b in range(2):
            turned = env[1, k, b].astype(F32).T.astype(BF16)
            rdiag[k, b * blk : (b + 1) * blk, b * blk : (b + 1) * blk] = turned
            rdiag[k, b * blk : (b + 1) * blk, (1 - b) * blk : (2 - b) * blk] = zeros
        return carry

    lax.fori_loop(0, chan, build_rdiag, 0)

    map_copy.wait()
    ranks_copy.wait()
    left_copy.wait()
    for k in range(chan):
        for b in range(2):
            lcat[b, :, k * blk : (k + 1) * blk] = env[0, k, b]

    def tiles(slab):
        return [slab[:, p * blk : (p + 1) * blk] for p in range(phys)]

    def contract(g):
        def one(k, carry):
            spots = [
                lax.rem(map_ref[0, 2 * group + b, k] + 4 - 2 * group, 4) for b in range(2)
            ]
            source = jnp.concatenate(
                [jnp.concatenate(tiles(x[g][spot]), axis=0) for spot in spots], axis=1
            )
            mixed = dot(kron[k], source).astype(BF16)
            part = dot(mixed, rdiag[k]).astype(BF16)
            row = pl.multiple_of(k * blk + g * rows, rows)
            for b in range(2):
                for p in range(phys):
                    z[b, pl.ds(row, rows), p * blk : (p + 1) * blk] = part[
                        p * rows : (p + 1) * rows, b * blk : (b + 1) * blk
                    ]
            return carry

        lax.fori_loop(0, chan, one, 0, unroll=7)

    def finish_image(b, num, keep_rounded):
        def one(n, carry):
            start = pl.multiple_of(n * 256, 256)
            cols = pl.ds(start, 256)
            tile = dot(lcat[b], z[b, :, cols])
            img[b, :, cols] = tile
            if keep_rounded:
                imgb[b, :, cols] = tile.astype(BF16)
            for g in range(chunks):
                part = x[g][b, :, cols].astype(F32) * tile[g * rows : (g + 1) * rows, :]
                carry = carry + part[:, :blk] + part[:, blk:]
            return carry

        return lax.fori_loop(0, wide // 256, one, num)

    def fold(product):
        both = product[0] + product[1]
        total = both[:, :blk]
        for p in range(1, phys):
            total = total + both[:, p * blk : (p + 1) * blk]
        return total

    def rows_of(g):
        return slice(g * rows, (g + 1) * rows)

    def send_sums(slot, parts):
        for i, part in enumerate(parts):
            sums[slot, i] = part
        copy = pltpu.make_async_remote_copy(
            src_ref=sums.at[slot, pl.ds(0, len(parts))],
            dst_ref=got.at[slot, pl.ds(0, len(parts))],
            send_sem=ss_sem.at[slot],
            recv_sem=sr_sem.at[slot],
            device_id=partner,
            device_id_type=MESH,
        )
        copy.start()
        return copy

    def total_of(part):
        return jnp.sum(part, axis=(0, 1), keepdims=True)

    den = jnp.zeros((rows, blk), F32)
    for g in range(chunks):
        own_copies[g].wait()
        own = x[g][0:2].astype(F32)
        den = den + fold(own * own)
        sends[g].wait_recv()
        contract(g)
    num = finish_image(0, jnp.zeros((rows, blk), F32), True)
    images = [[exchange_image(b, g) for g in range(chunks)] for b in range(2)]
    for g in range(2):
        images[0][g].start()
    num = finish_image(1, num, True)
    message = send_sums(0, [num, den])
    for g in range(2):
        images[1][g].start()
    for g in range(2, chunks):
        for b in range(2):
            images[b][g].start()
    message.wait()
    energy_one = total_of(num + got[0, 0]) / total_of(den + got[0, 1])

    den = jnp.zeros((rows, blk), F32)
    for g in range(chunks):
        own = x[g][0:2].astype(F32)
        first = (own - STEP_SIZE * (img[:, rows_of(g), :] - energy_one * own)).astype(BF16)
        x[g][0:2] = first
        first = first.astype(F32)
        den = den + fold(first * first)

    for g in range(chunks):
        for b in range(2):
            images[b][g].wait_recv()
        theirs = x[g][2:4].astype(F32)
        x[g][2:4] = (theirs - STEP_SIZE * (y[g][...].astype(F32) - energy_one * theirs)).astype(BF16)
        contract(g)
    num = jnp.zeros((rows, blk), F32)
    for b in range(2):
        num = finish_image(b, num, False)

    def quotient(top, bottom):
        top, bottom = total_of(top), total_of(bottom)
        return jnp.where(bottom > 0.0, top / bottom, 0.0)

    near = quotient(num, den)
    square = jnp.zeros((rows, blk), F32)
    cross = jnp.zeros((rows, blk), F32)
    start = jnp.zeros((rows, blk), F32)
    for g in range(chunks):
        line = g * rows + lax.broadcasted_iota(jnp.int32, (rows, wide), 0)
        first = x[g][0:2].astype(F32)
        first = jnp.stack(
            [jnp.where(line < ranks_ref[0, b], first[b], 0.0) for b in range(2)], axis=0
        )
        image = jnp.stack(
            [jnp.where(line < ranks_ref[0, b], img[b, rows_of(g), :], 0.0) for b in range(2)], axis=0
        )
        kept = first - STEP_SIZE * (image - near * first)
        img[:, rows_of(g), :] = kept
        square = square + fold(kept * kept)
        cross = cross + fold(kept * first)
        start = start + fold(first * first)
    send_sums(1, [num, den, square, cross, start]).wait()
    energy_two = total_of(num + got[1, 0]) / total_of(den + got[1, 1])

    def square_at(step, a, b, c):
        return total_of(a) + step * (0.5 * total_of(b) + 0.0625 * (step * total_of(c)))

    shift = energy_two - near
    far = energy_two - quotient(got[1, 0], got[1, 1])
    norm = square_at(shift, square, cross, start) + square_at(far, got[1, 2], got[1, 3], got[1, 4])
    norm = jnp.maximum(norm, 0.0)
    cells = float(4 * blk * wide)
    scale = jnp.sqrt(cells / (norm + EPSILON))
    for b in range(2):
        inside = lax.broadcasted_iota(jnp.int32, (blk, blk), 0) < ranks_ref[0, b]

        def turn(p, carry):
            cols = pl.ds(pl.multiple_of(p * blk, blk), blk)
            first = jnp.concatenate([x[g][b, :, cols] for g in range(chunks)], axis=0)
            first = jnp.where(inside, first.astype(F32), 0.0)
            tile = (img[b, :, cols] + (STEP_SIZE * shift) * first) * scale
            wave[0, b, :, cols] = tile.astype(BF16)
            wave[1, b, :, cols] = tile.T.astype(BF16)
            return carry

        lax.fori_loop(0, phys, turn, 0, unroll=2)
    new_copy = pltpu.make_async_copy(wave.at[0], new_ref.at[0], in_sem.at[2])
    new_copy.start()

    env_scale = 1.0 / math.sqrt(wide)
    first_side = 1 - lax.rem(seg, 2)

    def boundary(side, pair):
        channels = pl.ds(2 * pair, 2)
        target = lax.rem(seg + 1 - 2 * side + segs, segs)
        return pltpu.make_async_remote_copy(
            src_ref=outbuf.at[side, channels],
            dst_ref=recv_ref.at[side, channels],
            send_sem=es_sem.at[side, pair],
            recv_sem=er_sem.at[side, pair],
            device_id=(target, group),
            device_id_type=MESH,
        )

    for turn_index in range(2):
        side = first_side if turn_index == 0 else 1 - first_side

        def one_pair(pair, carry):
            for b in range(2):
                ends = jnp.concatenate([env[side, 2 * pair, b], env[side, 2 * pair + 1, b]], axis=0)
                for n in range(phys // 2):
                    part = dot(ends, wave[side, b, :, 2 * n * blk : (2 * n + 2) * blk]).astype(BF16)
                    for i in range(2):
                        for j in range(2):
                            mixbuf[
                                b,
                                (2 * n + j) * blk : (2 * n + j + 1) * blk,
                                i * blk : (i + 1) * blk,
                            ] = part[i * blk : (i + 1) * blk, j * blk : (j + 1) * blk]
            for b in range(2):
                result = (dot(wave[1 - side, b], mixbuf[b]) * env_scale).astype(BF16)
                for i in range(2):
                    outbuf[side, 2 * pair + i, b] = result[:, i * blk : (i + 1) * blk]
            boundary(side, pair).start()
            return carry

        lax.fori_loop(0, pairs, one_pair, 0)

    for copy in sends + images[0] + images[1]:
        copy.wait_send()
    new_copy.wait()

    def settle(pair, carry):
        for side in range(2):
            boundary(side, pair).wait()
        return carry

    lax.fori_loop(0, pairs, settle, 0)


def solution(mesh):
    segs = mesh.shape["seg"]

    def shards(state, left_env, right_env, site_ops, sector_map, ranks):
        chan, _, blk, _ = left_env.shape[1:]
        phys = site_ops.shape[2]
        rows = 16
        chunks = blk // rows
        wide = phys * blk
        dims = (segs, chan, phys, blk, rows, chunks)
        anywhere = pl.BlockSpec(memory_space=pl.ANY)
        dma = pltpu.SemaphoreType.DMA
        new_state, received = pl.pallas_call(
            functools.partial(kernel, dims),
            out_shape=(
                jax.ShapeDtypeStruct(state.shape, BF16),
                jax.ShapeDtypeStruct((2, chan, 2, blk, blk), BF16),
            ),
            in_specs=[anywhere] * 6,
            out_specs=(anywhere, anywhere),
            scratch_shapes=[pltpu.VMEM((4, rows, wide), BF16) for _ in range(chunks)]
            + [pltpu.VMEM((2, rows, wide), BF16) for _ in range(chunks)]
            + [
                pltpu.VMEM((2, chan, 2, blk, blk), BF16),
                pltpu.VMEM((2, blk, chan * blk), BF16),
                pltpu.VMEM((chan, phys * rows, phys * rows), BF16),
                pltpu.VMEM((chan, 2 * blk, 2 * blk), BF16),
                pltpu.VMEM((2, chan * blk, wide), BF16),
                pltpu.VMEM((2, blk, wide), F32),
                pltpu.VMEM((2, blk, wide), BF16),
                pltpu.VMEM((2, 2, blk, wide), BF16),
                pltpu.VMEM((2, wide, 2 * blk), BF16),
                pltpu.VMEM((2, chan, 2, blk, blk), BF16),
                pltpu.VMEM((2, 5, rows, blk), F32),
                pltpu.VMEM((2, 5, rows, blk), F32),
                pltpu.VMEM((chan, phys, phys), BF16),
                pltpu.SMEM((1, 4, chan), jnp.int32),
                pltpu.SMEM((1, 2), jnp.int32),
                dma((6,)),
                dma((chunks,)),
                dma((chunks,)),
                dma((chunks,)),
                dma((2, chunks)),
                dma((2, chunks)),
                dma((2, chan // 2)),
                dma((2, chan // 2)),
                dma((2,)),
                dma((2,)),
            ],
            compiler_params=pltpu.CompilerParams(
                collective_id=0, has_side_effects=True, vmem_limit_bytes=60 * 1024 * 1024
            ),
        )(state, left_env, right_env, site_ops, jnp.swapaxes(sector_map, 1, 2), ranks)
        seg = lax.axis_index("seg")
        from_left = jnp.where(seg == 0, 0.0, received[0].astype(F32))
        from_right = jnp.where(seg == segs - 1, 0.0, received[1].astype(F32))
        return (new_state, from_left[None], from_right[None])

    placed = (
        P("seg", "blk", None, None),
        P("seg", None, "blk", None, None),
        P("seg", None, "blk", None, None),
        P("seg", None, None, None),
        P("seg", None, None),
        P("seg", "blk"),
    )
    return jax.shard_map(
        shards,
        mesh=mesh,
        in_specs=placed,
        out_specs=(
            P("seg", "blk", None, None),
            P("seg", None, "blk", None, None),
            P("seg", None, "blk", None, None),
        ),
        check_vma=False,
    )
```
